256 devices in a mesh: term: 8 (over y, core), pass: 32 (over x, z).
Axes of the slice: x: 4, y: 4, z: 8, core: 2. Of those that a mesh axis runs over, the one named last changes fastest.
Arguments:
- hidden: bfloat16 [16384, 4096], P('pass', 'term'), may hold values from -16 to 16
- head_weight: bfloat16 [4096, 16384], P('pass', 'term'), may hold values from -0.09375 to 0.09375
- lengths: int32 [256], P('pass'), may hold values from 1 to 64, as said below
Outputs:
- postings: bfloat16 [16384, 256], P(('term', 'pass'))
The draws below stay inside these ranges and needn't reach their ends.
Inputs may be any that keep to these rules, and one draw needn't show every extreme that they name: Passage p's valid tokens are its first lengths[p] slots; some passage has exactly 64.
All inputs are finite; a program needn't handle non-finite values.
Results may differ from the reference program's by a relative error of at most 0.013.
Values may be sent and summed in bfloat16 or wider, within the bound.
No kernel may reach another device: no remote copies, remote signals or barrier semaphores. Data moves between devices by JAX's collectives and lax.ppermute only.
A program may use at most 64 MiB of HBM per device.

```python
import jax
import jax.numpy as jnp
from jax import lax

D = 4096
VW = 16384
LEN = 64
PASSAGES = 256
TOKENS = 16384


def draw_hidden(key, part):
    first, second = jax.random.split(key, 2)
    owners = jnp.arange(TOKENS, dtype=jnp.int32) // LEN
    rising = jnp.float32(3.0) ** (owners.astype(jnp.float32) / jnp.float32(max(PASSAGES - 1, 1)))
    values = jax.random.normal(first, (TOKENS, D), jnp.float32)
    jitter = jnp.exp(jax.random.uniform(second, (TOKENS, 1), jnp.float32, -0.55, 0.55))
    result = values * jitter * 0.8 * rising[:, None]
    return jnp.clip(result, -16.0, 16.0).astype(jnp.bfloat16)


def draw_lengths(key, part):
    first, second, third = jax.random.split(key, 3)
    counts = jax.random.randint(first, (PASSAGES,), 1, LEN + 1, dtype=jnp.int32)
    longest = jax.random.randint(second, (), 0, PASSAGES, dtype=jnp.int32)
    shortest = (longest + jax.random.randint(third, (), 1, PASSAGES, dtype=jnp.int32)) % PASSAGES
    places = jnp.arange(PASSAGES, dtype=jnp.int32)
    counts = jnp.where(places == longest, LEN, jnp.where(places == shortest, 1, counts))
    return counts.astype(jnp.int32)


def block_levels(own_key, dims, shards, smallest, high):
    factor_of = 1.0
    for position, blocks in shards:
        steps = jax.random.uniform(jax.random.fold_in(jax.random.fold_in(own_key, 6), position), (blocks,), jnp.float32, smallest / len(shards), high / len(shards))
        factor_of = factor_of * jnp.repeat(jnp.exp(steps), dims[position] // blocks).reshape((-1,) + (1,) * (len(dims) - 1 - position))
    return factor_of


def noise(key, extent, width, reach, cuts=(), held_as=jnp.bfloat16):
    level = block_levels(key, extent, cuts, -0.22, 0.18) if cuts else 1.0
    drawn = jax.random.normal(key, extent, jnp.float32) * width * level
    return jnp.minimum(jnp.maximum(drawn, -reach), reach).astype(held_as)


def setup_inputs(seed: int = 0) -> dict:
    keys = jax.random.split(jax.random.key(seed), 4)
    return {
        "hidden": draw_hidden(jax.random.fold_in(keys[3], 71), 0),
        "head_weight": noise(keys[1], (D, VW), D ** -0.5, 0.09375, ((0, 32), (1, 8))),
        "lengths": draw_lengths(jax.random.fold_in(keys[3], 71), 0),
    }


def reference(hidden, head_weight, lengths):
    block_cols = min(VW, 1024)
    positions = jnp.arange(LEN, dtype=jnp.int32)
    allowed = positions[None, :] < lengths[:, None]
    weight_blocks = head_weight.reshape(D, VW // block_cols, block_cols).transpose(1, 0, 2)

    def pooling(weight_block):
        logits = jnp.dot(hidden, weight_block, preferred_element_type=jnp.float32)
        impacts = jnp.log1p(jnp.maximum(logits, jnp.float32(0.0))).reshape(PASSAGES, LEN, block_cols)
        impacts = jnp.where(allowed[:, :, None], impacts, jnp.float32(0.0))
        return jnp.max(impacts, axis=1).astype(jnp.bfloat16)

    pooled = lax.map(pooling, weight_blocks)
    pooled = pooled.transpose(1, 0, 2).reshape(PASSAGES, VW)
    pooled_f = pooled.astype(jnp.float32)
    column_max = jnp.max(pooled_f, axis=0)
    scaled = pooled_f / (1.0 + column_max)[None, :]
    return scaled.T.astype(jnp.bfloat16)
```

```python
import functools

import jax
import jax.numpy as jnp
from jax import lax
from jax.experimental import pallas as pl
from jax.experimental.pallas import tpu as pltpu
from jax.sharding import Mesh, PartitionSpec as P

LEN = 64


def pool_kernel(where, a_ref, *refs):
    nz = where.shape[0]
    pieces, (o_ref, w, sems) = refs[:nz], refs[nz:]
    nx, rows = pieces[0].shape[0], pieces[0].shape[1]

    def copies():
        for s in range(nz):
            at = where[s] * rows
            for i in range(nx):
                to = pl.multiple_of(at + i * nz * rows, rows)
                yield pltpu.make_async_copy(
                    pieces[s].at[i], w.at[pl.ds(to, rows)], sems.at[s, i]
                )

    @pl.when(pl.program_id(0) == 0)
    def _():
        for c in copies():
            c.start()
        for c in copies():
            c.wait()

    depth = a_ref.shape[2]
    acc = jnp.dot(a_ref[0], w[:depth], preferred_element_type=jnp.float32)
    for k in range(1, a_ref.shape[0]):
        acc += jnp.dot(
            a_ref[k],
            w[k * depth : (k + 1) * depth],
            preferred_element_type=jnp.float32,
        )
    tokens, cols = acc.shape
    top = jnp.max(acc.reshape(tokens // LEN, LEN, cols), axis=1)
    o_ref[...] = jnp.log1p(jnp.maximum(top, 0.0)).astype(o_ref.dtype)


def pool(where, gathered, pieces, nx):
    blocks, tokens, depth = gathered.shape
    cols = pieces[0].shape[-1]
    per = blocks // nx
    nz = len(pieces)
    return pl.pallas_call(
        pool_kernel,
        out_shape=jax.ShapeDtypeStruct((nx * tokens // LEN, cols), jnp.bfloat16),
        grid_spec=pltpu.PrefetchScalarGridSpec(
            num_scalar_prefetch=1,
            grid=(nx,),
            in_specs=[pl.BlockSpec((per, tokens, depth), lambda i, _: (i, 0, 0))]
            + [pl.BlockSpec(memory_space=pl.ANY)] * nz,
            out_specs=pl.BlockSpec((tokens // LEN, cols), lambda i, _: (i, 0)),
            scratch_shapes=[
                pltpu.VMEM((per * depth, cols), jnp.bfloat16),
                pltpu.SemaphoreType.DMA((nz, nx)),
            ],
        ),
        compiler_params=pltpu.CompilerParams(vmem_limit_bytes=48 << 20),
    )(where, gathered, *pieces)


def ring(block, axis):
    n = lax.axis_size(axis)
    up = [(i, (i + 1) % n) for i in range(n)]
    down = [(i, (i - 1) % n) for i in range(n)]
    out, offsets = [block], [0]
    low = high = block
    for s in range(1, n // 2):
        low = lax.ppermute(low, axis, up)
        high = lax.ppermute(high, axis, down)
        out += [low, high]
        offsets += [-s, s]
    out.append(lax.ppermute(low, axis, up))
    offsets.append(-(n // 2))
    return out, offsets


def body(hidden, head_weight, lengths):
    nx, nz = lax.axis_size("x"), lax.axis_size("z")
    z = lax.axis_index("z")
    rows, cols = head_weight.shape
    per = hidden.shape[0] // lengths.shape[0]
    allowed = jnp.arange(per, dtype=jnp.int32)[None, :] < lengths[:, None]
    hidden = jnp.where(
        allowed[:, :, None], hidden.reshape(-1, per, hidden.shape[1]), 0
    ).reshape(hidden.shape)
    full = lax.all_gather(hidden, ("x", "y", "c"), axis=0, tiled=False)
    head = head_weight.reshape(rows, nx, cols // nx)
    head = lax.all_to_all(head, "x", split_axis=1, concat_axis=0, tiled=False)
    head = head.reshape(nx, rows, cols // nx)
    pieces, offsets = ring(head, "z")
    where = (z + jnp.array(offsets, jnp.int32) + nz) % nz
    pooled = pool(where, full.reshape(-1, *hidden.shape), pieces, nx)
    pooled = pooled.reshape(nx, -1, nz, pooled.shape[1] // nz)
    mine = lax.all_to_all(pooled, "z", split_axis=2, concat_axis=1, tiled=False)
    mine = mine.reshape(-1, mine.shape[-1]).astype(jnp.float32)
    peak = jnp.max(mine, axis=0)
    return jnp.transpose((mine / (1.0 + peak)[None, :]).astype(jnp.bfloat16))


def solution(mesh):
    fine = Mesh(mesh.devices.reshape(4, 2, 4, 8), ("y", "c", "x", "z"))
    return jax.shard_map(
        body,
        mesh=fine,
        in_specs=(P(("x", "z"), ("y", "c")), P(("x", "z"), ("y", "c")), P(("x", "z"))),
        out_specs=P(("y", "c", "x", "z"), None),
        check_vma=False,
    )
```

```python
import jax
import jax.numpy as jnp
from jax import lax
from jax.experimental import pallas as pl
from jax.experimental.pallas import tpu as pltpu
from jax.sharding import Mesh, PartitionSpec as P

LEN = 64
AXES = ("y", "c", "x", "z")
NY, NC, NX, NZ = SIZES = (4, 2, 4, 8)


def permute(block, move):
    pairs = []
    for y in range(NY):
        for c in range(NC):
            for x in range(NX):
                for z in range(NZ):
                    to = [a % n for a, n in zip(move(y, c, x, z), SIZES)]
                    pairs.append(
                        (
                            ((y * NC + c) * NX + x) * NZ + z,
                            ((to[0] * NC + to[1]) * NX + to[2]) * NZ + to[3],
                        )
                    )
    return lax.ppermute(block, AXES, pairs)


def swap(block):
    return permute(block, lambda y, c, x, z: (y, 1 - c, x, z))


def first(block, s):
    return permute(
        block, lambda y, c, x, z: (y + s, c, x, z) if c == 0 else (y, c, x + s, z)
    )


def second(block, s):
    return permute(
        block, lambda y, c, x, z: (y, c, x + s, z) if c == 0 else (y + s, c, x, z)
    )


def along_z(block):
    return permute(
        block, lambda y, c, x, z: (y, c, x, z + 1) if c == 0 else (y, c, x, z - 1)
    )


def gather_hidden(own):
    lower = first(own, 1)
    upper = first(own, -1)
    three = jnp.concatenate([own, lower, upper], axis=0)
    far = first(upper, -1)
    three_lower = second(three, 1)
    three_upper = second(three, -1)
    far_lower = second(far, 1)
    far_upper = second(far, -1)
    three_far = second(three_lower, 1)
    far_far = second(far_upper, -1)
    return [
        (three, 0),
        (far, 0),
        (three_lower, -1),
        (three_upper, 1),
        (far_lower, -1),
        (far_upper, 1),
        (three_far, 2),
        (far_far, 2),
    ]


def gather_head(piece):
    own = jnp.stack([piece, swap(piece)])
    out = [(own, 0, True)]
    block = own
    for s in range(1, NZ // 2):
        block = along_z(block)
        out += [(block, -s, True), (swap(block), s, False)]
    last = along_z(block[:1])
    out += [(last, NZ // 2, True), (swap(last), NZ // 2, False)]
    return out


def pool_kernel(units, parts, place, *refs):
    n, m = len(units), len(parts)
    hid, head, (o_ref, w, acc) = refs[:n], refs[n : n + m], refs[n + m :]
    y, c, x, z = (place[i] for i in range(4))
    for ref, (steps, mine) in zip(head, parts):
        sign = 1 - 2 * c
        at_z = lax.rem(z + sign * steps + NZ, NZ)
        rows = ref.shape[2]
        for q in range(ref.shape[0]):
            col = c if (q == 0) == mine else 1 - c

            def place_rows(i, _):
                at_x = lax.rem(x - i + NX, NX)
                to = pl.multiple_of((at_x * NZ + at_z) * rows, rows)
                w[col, pl.ds(to, rows), :] = ref[q, i]
                return 0

            lax.fori_loop(0, NX, place_rows, 0)
    acc[...] = jnp.zeros_like(acc)
    depth = hid[0].shape[-1]
    for ref, b in zip(hid, units):

        def unit(u, _):
            a = jnp.where(u == 2, 1, -u) if ref.shape[0] > 1 else 2
            at_y = lax.rem(y + jnp.where(c == 0, a, b) + NY, NY)
            at_x = lax.rem(x + jnp.where(c == 0, b, a) + NX, NX)
            for col in range(NC):
                total = acc[at_x, :, col * w.shape[2] : (col + 1) * w.shape[2]]
                for h in range(NC):
                    f = c if h == 0 else 1 - c
                    row = pl.multiple_of((at_y * NC + f) * depth, depth)
                    total += jnp.dot(
                        ref[u, h],
                        w[col, pl.ds(row, depth), :],
                        preferred_element_type=jnp.float32,
                    )
                acc[at_x, :, col * w.shape[2] : (col + 1) * w.shape[2]] = total
            return 0

        lax.fori_loop(0, ref.shape[0], unit, 0)
    for i in range(NX):
        tokens, cols = acc.shape[1:]
        top = jnp.max(acc[i].reshape(tokens // LEN, LEN, cols), axis=1)
        o_ref[i] = jnp.log1p(jnp.maximum(top, 0.0))


def pool(place, hid, head):
    tokens, depth = hid[0][0].shape[-2:]
    rows, cols = head[0][0].shape[-2:]
    whole = pl.BlockSpec(memory_space=pltpu.VMEM)
    arrays = [h[0] for h in hid] + [h[0] for h in head]

    def kernel(*refs):
        pool_kernel([h[1] for h in hid], [h[1:] for h in head], *refs)

    return pl.pallas_call(
        kernel,
        out_shape=jax.ShapeDtypeStruct((NX, tokens // LEN, NC * cols), jnp.float32),
        in_specs=[pl.BlockSpec(memory_space=pltpu.SMEM)] + [whole] * len(arrays),
        out_specs=whole,
        scratch_shapes=[
            pltpu.VMEM((NC, NX * NZ * rows, cols), jnp.bfloat16),
            pltpu.VMEM((NX, tokens, NC * cols), jnp.float32),
        ],
        compiler_params=pltpu.CompilerParams(vmem_limit_bytes=50 << 20),
    )(place, *arrays)


def body(hidden, head_weight, lengths):
    y, c, x, z = (lax.axis_index(a) for a in AXES)
    tokens, features = hidden.shape
    rows, cols = head_weight.shape
    per = tokens // lengths.shape[0]
    allowed = jnp.arange(per, dtype=jnp.int32)[None, :] < lengths[:, None]
    hidden = jnp.where(
        allowed[:, :, None], hidden.reshape(-1, per, features), 0
    ).reshape(NC, tokens // NC, features)
    kept = lax.dynamic_index_in_dim(hidden, c, 0, keepdims=False)
    other = swap(lax.dynamic_index_in_dim(hidden, 1 - c, 0, keepdims=False))
    units = gather_hidden(jnp.stack([kept, other])[None])

    width = cols // NX
    mine = [lax.dynamic_slice(head_weight, (0, x * width), (rows, width))]
    for s in range(1, NX):
        to = lax.rem(x + s, NX)
        block = lax.dynamic_slice(head_weight, (0, to * width), (rows, width))
        mine.append(permute(block, lambda y, c, x, z: (y, c, x + s, z)))
    parts = gather_head(jnp.stack(mine))

    place = jnp.stack([y, c, x, z]).astype(jnp.int32)
    pooled = pool(place, units, parts).astype(jnp.bfloat16)
    each = width // NZ
    pooled = pooled.reshape(NX * pooled.shape[1], NC, NZ, each)
    pooled = jnp.transpose(pooled, (2, 1, 0, 3)).reshape(NZ * NC, -1, each)
    got = lax.all_to_all(pooled, ("z", "c"), split_axis=0, concat_axis=0, tiled=True)
    got = got.reshape(NZ, NC, NX, -1, each)
    got = jnp.transpose(got, (2, 0, 1, 3, 4)).reshape(-1, each).astype(jnp.float32)
    peak = jnp.max(got, axis=0)
    return jnp.transpose((got / (1.0 + peak)[None, :]).astype(jnp.bfloat16))


def solution(mesh):
    fine = Mesh(mesh.devices.reshape(SIZES), AXES)
    return jax.shard_map(
        body,
        mesh=fine,
        in_specs=(P(("x", "z"), ("y", "c")), P(("x", "z"), ("y", "c")), P(("x", "z"))),
        out_specs=P(("y", "c", "x", "z"), None),
        check_vma=False,
    )
```

```python
import jax
import jax.numpy as jnp
from jax import lax
from jax.experimental import pallas as pl
from jax.experimental.pallas import tpu as pltpu
from jax.sharding import Mesh, PartitionSpec as P

LEN = 64
AXES = ("y", "c", "x", "z")
NY, NC, NX, NZ = SIZES = (4, 2, 4, 8)
VMEM = pl.BlockSpec(memory_space=pltpu.VMEM)
SMEM = pl.BlockSpec(memory_space=pltpu.SMEM)


def permute(block, move):
    pairs = []
    for y in range(NY):
        for c in range(NC):
            for x in range(NX):
                for z in range(NZ):
                    to = [a % n for a, n in zip(move(y, c, x, z), SIZES)]
                    pairs.append(
                        (
                            ((y * NC + c) * NX + x) * NZ + z,
                            ((to[0] * NC + to[1]) * NX + to[2]) * NZ + to[3],
                        )
                    )
    return lax.ppermute(block, AXES, pairs)


def swap(block):
    return permute(block, lambda y, c, x, z: (y, 1 - c, x, z))


def first(block, s):
    return permute(
        block, lambda y, c, x, z: (y + s, c, x, z) if c == 0 else (y, c, x + s, z)
    )


def second(block, s):
    return permute(
        block, lambda y, c, x, z: (y, c, x + s, z) if c == 0 else (y + s, c, x, z)
    )


def along_z(block):
    return permute(
        block, lambda y, c, x, z: (y, c, x, z + 1) if c == 0 else (y, c, x, z - 1)
    )


def prep_kernel(place, lengths, hid, head, kept, other, *blocks):
    c, x = place[1], place[2]
    half, width = kept.shape[0], blocks[0].shape[1]
    for out, part in ((kept, c), (other, 1 - c)):
        for p in range(half // LEN):
            n = lengths[part * (half // LEN) + p]
            at = pl.multiple_of(part * half + p * LEN, LEN)
            rows = hid[pl.ds(at, LEN), :]
            j = lax.broadcasted_iota(jnp.int32, rows.shape, 0)
            zero = jnp.zeros_like(rows)
            out[p * LEN : (p + 1) * LEN, :] = jnp.where(j < n, rows, zero)
    for s, out in enumerate(blocks):
        at = pl.multiple_of(lax.rem(x + s, NX) * width, width)
        out[...] = head[:, pl.ds(at, width)]


def prep(place, lengths, hidden, head):
    half = jax.ShapeDtypeStruct((hidden.shape[0] // NC, hidden.shape[1]), hidden.dtype)
    block = jax.ShapeDtypeStruct((head.shape[0], head.shape[1] // NX), head.dtype)
    return pl.pallas_call(
        prep_kernel,
        out_shape=[half, half] + [block] * NX,
        in_specs=[SMEM, SMEM, VMEM, VMEM],
        out_specs=[VMEM] * (2 + NX),
    )(place, lengths, hidden, head)


ORDER = (
    ("h0", ()),
    ("x1", ()),
    ("x3", ()),
    ("x2", ()),
    ("f-", ("h0",)),
    ("f+", ()),
    ("sU-", ("x1",)),
    ("A1", ("x2", "x3")),
    ("sU+", ()),
    ("b0", ("f-",)),
    ("ff", ("f+",)),
    ("B1", ("b0",)),
    ("sP-", ("sU-",)),
    ("A2", ("A1",)),
    ("sP+", ("sU+",)),
    ("B2", ("B1",)),
    ("cB1", ("ff",)),
    ("sF-", ("cB1",)),
    ("A3", ("A2",)),
    ("cA2", ("sP-",)),
    ("sF+", ("cA2",)),
    ("B3", ("B2",)),
    ("gU", ("sP+",)),
    ("gP", ("sF-",)),
    ("A4", ("A3",)),
    ("gF", ("sF+",)),
    ("cB3", ("B3",)),
    ("cB2", ("gU",)),
    ("cA3", ("cB3",)),
    ("cA1", ("cB2",)),
    ("cA4", ("A4",)),
)


def exchange(kept, other, blocks):
    got = {"kept": kept, "other": other}

    def own():
        if "own" not in got:
            got["own"] = jnp.stack([kept, got["h0"]])[None]
        return got["own"]

    def pair():
        if "pair" not in got:
            got["pair"] = jnp.concatenate([got["f+"], got["f-"]], axis=0)
        return got["pair"]

    def piece():
        if "A0" not in got:
            got["A0"] = jnp.stack([blocks[0], got["x1"], got["x2"], got["x3"]])
        return got["A0"]

    def across(s):
        return lambda b: permute(b, lambda y, c, x, z: (y, c, x + s, z))

    moves = {
        "h0": (swap, lambda: other),
        "x1": (across(1), lambda: blocks[1]),
        "x2": (across(2), lambda: blocks[2]),
        "x3": (across(3), lambda: blocks[3]),
        "f+": (lambda b: first(b, 1), own),
        "f-": (lambda b: first(b, -1), own),
        "ff": (lambda b: first(b, 1), lambda: got["f+"]),
        "sU+": (lambda b: second(b, 1), own),
        "sU-": (lambda b: second(b, -1), own),
        "sP+": (lambda b: second(b, 1), pair),
        "sP-": (lambda b: second(b, -1), pair),
        "sF+": (lambda b: second(b, 1), lambda: got["ff"]),
        "sF-": (lambda b: second(b, -1), lambda: got["ff"]),
        "gU": (lambda b: second(b, -1), lambda: got["sU-"]),
        "gP": (lambda b: second(b, 1), lambda: got["sP+"]),
        "gF": (lambda b: second(b, -1), lambda: got["sF-"]),
        "b0": (swap, piece),
        "A1": (along_z, piece),
        "B1": (along_z, lambda: got["b0"]),
        "A2": (along_z, lambda: got["A1"]),
        "B2": (along_z, lambda: got["B1"]),
        "A3": (along_z, lambda: got["A2"]),
        "B3": (along_z, lambda: got["B2"]),
        "A4": (along_z, lambda: got["A3"]),
    }
    for n in ("A1", "B1", "A2", "B2", "A3", "B3", "A4"):
        moves["c" + n] = (swap, lambda n=n: got[n])
    for name, arrived in ORDER:
        move, operand = moves[name]
        block = operand()
        if arrived:
            block = lax.optimization_barrier((block, *(got[a] for a in arrived)))[0]
        got[name] = move(block)
    return got


def hidden_blocks(got):
    return [
        (got["own"], 0, 0),
        (got["sU+"], 0, -1),
        (got["sU-"], 0, 1),
        (got["pair"], None, 0),
        (got["ff"], 2, 0),
        (got["gU"], 0, 2),
        (got["sP+"], None, -1),
        (got["sP-"], None, 1),
        (got["sF+"], 2, -1),
        (got["sF-"], 2, 1),
        (got["gF"], 2, 2),
        (got["gP"], None, 2),
    ]


def head_pieces(got):
    mine, theirs, steps = [got["A0"]], [got["b0"]], [0]
    for s in ("1", "2", "3"):
        mine += [got["A" + s], got["cB" + s]]
        theirs += [got["B" + s], got["cA" + s]]
        steps += [-int(s), int(s)]
    return mine + [got["A4"]], theirs + [got["cA4"]], steps + [NZ // 2]


def pool_kernel(units, steps, place, *refs):
    n, m = len(units), len(steps)
    hid, head = refs[:n], (refs[n : n + m], refs[n + m : n + 2 * m])
    o_ref, acc = refs[n + 2 * m :]
    y, c, x, z = (place[i] for i in range(4))
    rows = head[0][0].shape[1]
    per = hid[0].shape[-1] // rows
    from_z = [lax.rem(z + (1 - 2 * c) * s + NZ, NZ) for s in steps]
    halves = [jnp.where(lax.div(f, per) == c, 0, 1) for f in from_z]
    lanes = [pl.multiple_of(lax.rem(f, per) * rows, rows) for f in from_z]
    acc[...] = jnp.zeros_like(acc)
    for ref, (a, b) in zip(hid, units):

        def unit(u, _):
            along = 2 * u - 1 if a is None else a
            at_y = lax.rem(y + jnp.where(c == 0, along, b) + NY, NY)
            at_x = lax.rem(x + jnp.where(c == 0, b, along) + NX, NX)
            i = lax.rem(x - at_y + NX, NX)
            left = jnp.concatenate(
                [ref[u, h, :, pl.ds(at, rows)] for h, at in zip(halves, lanes)], axis=1
            )
            for col in range(NC):
                right = jnp.concatenate([p[i] for p in head[col]], axis=0)
                acc[col, at_x] += jnp.dot(
                    left, right, preferred_element_type=jnp.float32
                )
            return 0

        lax.fori_loop(0, ref.shape[0], unit, 0)
    for col in range(NC):
        for i in range(NX):
            tokens, cols = acc.shape[2:]
            top = jnp.max(acc[col, i].reshape(tokens // LEN, LEN, cols), axis=1)
            o_ref[lax.rem(c + col, NC), i] = jnp.log1p(jnp.maximum(top, 0.0))


def pool(place, hid, head):
    mine, theirs, steps = head
    tokens = hid[0][0].shape[-2]
    cols = mine[0].shape[-1]
    arrays = [h[0] for h in hid] + mine + theirs

    def kernel(*refs):
        pool_kernel([h[1:] for h in hid], steps, *refs)

    return pl.pallas_call(
        kernel,
        out_shape=jax.ShapeDtypeStruct((NC, NX, tokens // LEN, cols), jnp.float32),
        in_specs=[SMEM] + [VMEM] * len(arrays),
        out_specs=VMEM,
        scratch_shapes=[pltpu.VMEM((NC, NX, tokens, cols), jnp.float32)],
        compiler_params=pltpu.CompilerParams(vmem_limit_bytes=14 << 20),
    )(place, *arrays)


def body(hidden, head_weight, lengths):
    place = jnp.stack([lax.axis_index(a) for a in AXES]).astype(jnp.int32)
    kept, other, *blocks = prep(place, lengths, hidden, head_weight)
    got = exchange(kept, other, blocks)
    pooled = pool(place, hidden_blocks(got), head_pieces(got)).astype(jnp.bfloat16)
    each = pooled.shape[-1] // NZ
    pooled = pooled.reshape(NC, NX * pooled.shape[2], NZ, each)
    pooled = jnp.transpose(pooled, (2, 0, 1, 3)).reshape(NZ * NC, -1, each)
    got = lax.all_to_all(pooled, ("z", "c"), split_axis=0, concat_axis=0, tiled=True)
    got = got.reshape(NZ, NC, NX, -1, each)
    got = jnp.transpose(got, (2, 0, 1, 3, 4)).reshape(-1, each).astype(jnp.float32)
    peak = jnp.max(got, axis=0)
    return jnp.transpose((got / (1.0 + peak)[None, :]).astype(jnp.bfloat16))


def solution(mesh):
    fine = Mesh(mesh.devices.reshape(SIZES), AXES)
    return jax.shard_map(
        body,
        mesh=fine,
        in_specs=(P(("x", "z"), ("y", "c")), P(("x", "z"), ("y", "c")), P(("x", "z"))),
        out_specs=P(("y", "c", "x", "z"), None),
        check_vma=False,
    )
```

```python
import jax
import jax.numpy as jnp
from jax import lax
from jax.experimental import pallas as pl
from jax.experimental.pallas import tpu as pltpu
from jax.sharding import Mesh, PartitionSpec as P

LEN = 64
AXES = ("y", "c", "x", "z")
NY, NC, NX, NZ = SIZES = (4, 2, 4, 8)
VMEM = pl.BlockSpec(memory_space=pltpu.VMEM)
SMEM = pl.BlockSpec(memory_space=pltpu.SMEM)


def permute(block, move):
    pairs = []
    for y in range(NY):
        for c in range(NC):
            for x in range(NX):
                for z in range(NZ):
                    to = [a % n for a, n in zip(move(y, c, x, z), SIZES)]
                    pairs.append(
                        (
                            ((y * NC + c) * NX + x) * NZ + z,
                            ((to[0] * NC + to[1]) * NX + to[2]) * NZ + to[3],
                        )
                    )
    return lax.ppermute(block, AXES, pairs)


def swap(block):
    return permute(block, lambda y, c, x, z: (y, 1 - c, x, z))


def first(block, s):
    return permute(
        block, lambda y, c, x, z: (y + s, c, x, z) if c == 0 else (y, c, x + s, z)
    )


def second(block, s):
    return permute(
        block, lambda y, c, x, z: (y, c, x + s, z) if c == 0 else (y + s, c, x, z)
    )


def along_z(block):
    return permute(
        block, lambda y, c, x, z: (y, c, x, z + 1) if c == 0 else (y, c, x, z - 1)
    )


def across_z(block):
    return permute(
        block, lambda y, c, x, z: (y, 0, x, z + 1) if c == 1 else (y, 1, x, z - 1)
    )


def prep_kernel(place, lengths, hid, head, kept, other, blocks):
    c = place[1]
    half, width = kept.shape[0], blocks.shape[2]
    for out, part in ((kept, c), (other, 1 - c)):
        for p in range(half // LEN):
            n = lengths[part * (half // LEN) + p]
            at = pl.multiple_of(part * half + p * LEN, LEN)
            rows = hid[pl.ds(at, LEN), :]
            j = lax.broadcasted_iota(jnp.int32, rows.shape, 0)
            zero = jnp.zeros_like(rows)
            out[p * LEN : (p + 1) * LEN, :] = jnp.where(j < n, rows, zero)
    for s in range(blocks.shape[0]):
        blocks[s] = head[:, s * width : (s + 1) * width]


def prep(place, lengths, hidden, head):
    rows, cols = head.shape
    half = jax.ShapeDtypeStruct((hidden.shape[0] // NC, hidden.shape[1]), hidden.dtype)
    blocks = jax.ShapeDtypeStruct((NX, rows, cols // NX), head.dtype)
    return pl.pallas_call(
        prep_kernel,
        out_shape=[half, half, blocks],
        in_specs=[SMEM, SMEM, VMEM, VMEM],
        out_specs=[VMEM] * 3,
        compiler_params=pltpu.CompilerParams(vmem_limit_bytes=6 << 20),
    )(place, lengths, hidden, head)


ORDER = (
    ("h0", ()),
    ("f+", ()),
    ("f-", ()),
    ("A1", ("f+", "f-")),
    ("B1", ("f+", "f-")),
    ("sP+", ()),
    ("sP-", ()),
    ("ff", ()),
    ("sU-", ()),
    ("sU+", ()),
    ("A2", ("sU+", "sU-")),
    ("B2", ()),
    ("sF-", ()),
    ("gP", ()),
    ("A3", ("sP+", "sP-", "ff")),
    ("B3", ("sF-",)),
    ("B0", ("A1",)),
    ("c1", ()),
    ("gF", ()),
    ("sF+", ()),
    ("gU", ()),
    ("c2", ("c1", "B0")),
    ("A4", ("gU",)),
    ("c3", ("gP", "gF", "sum1")),
    ("c4", ("sF+", "c2", "c3", "sum2")),
)


def exchange(place, kept, other, blocks):
    got = {"kept": kept, "other": other}

    def own():
        if "own" not in got:
            got["own"] = jnp.stack([kept, got["h0"]])[None]
        return got["own"]

    def pair():
        if "pair" not in got:
            got["pair"] = jnp.concatenate([got["f+"], got["f-"]], axis=0)
        return got["pair"]

    def piece():
        if "A0" not in got:
            got["A0"] = lax.all_to_all(blocks, "x", split_axis=0, concat_axis=0)
        return got["A0"]

    moves = {
        "h0": (swap, lambda: other),
        "f+": (lambda b: first(b, 1), own),
        "f-": (lambda b: first(b, -1), own),
        "ff": (lambda b: first(b, 1), lambda: got["f+"]),
        "sU+": (lambda b: second(b, 1), own),
        "sU-": (lambda b: second(b, -1), own),
        "sP+": (lambda b: second(b, 1), pair),
        "sP-": (lambda b: second(b, -1), pair),
        "sF+": (lambda b: second(b, 1), lambda: got["ff"]),
        "sF-": (lambda b: second(b, -1), lambda: got["ff"]),
        "gU": (lambda b: second(b, -1), lambda: got["sU-"]),
        "gP": (lambda b: second(b, 1), lambda: got["sP+"]),
        "gF": (lambda b: second(b, -1), lambda: got["sF-"]),
        "B0": (swap, piece),
        "A1": (along_z, piece),
        "B1": (across_z, piece),
        "A2": (along_z, lambda: got["A1"]),
        "B2": (along_z, lambda: got["B1"]),
        "A3": (along_z, lambda: got["A2"]),
        "B3": (along_z, lambda: got["B2"]),
        "A4": (along_z, lambda: got["A3"]),
    }
    moves["c4"] = (swap, lambda: got["A4"])
    for n in "123":
        moves["c" + n] = (swap, lambda n=n: jnp.stack([got["A" + n], got["B" + n]]))
    for name, arrived in ORDER:
        for k in range(len(STAGES)):
            if "sum%d" % (k + 1) in arrived:
                got["sum%d" % (k + 1)] = run_stage(k, place, got)
        move, operand = moves[name]
        block = operand()
        if arrived:
            block = lax.optimization_barrier((block, *(got[a] for a in arrived)))[0]
        got[name] = move(block)
    for k in range(len(STAGES)):
        if "sum%d" % (k + 1) not in got:
            got["sum%d" % (k + 1)] = run_stage(k, place, got)
    return got["sum%d" % len(STAGES)]


STEPS = {
    "own": (0, 0),
    "sU+": (0, -1),
    "sU-": (0, 1),
    "pair": (None, 0),
    "ff": (2, 0),
    "gU": (0, 2),
    "sP+": (None, -1),
    "sP-": (None, 1),
    "sF+": (2, -1),
    "sF-": (2, 1),
    "gF": (2, 2),
    "gP": (None, 2),
}
PIECES = {
    0: ("A0", "B0"),
    -1: ("A1", "B1"),
    1: ("c1", "c1"),
    -2: ("A2", "B2"),
    2: ("c2", "c2"),
    -3: ("A3", "B3"),
    3: ("c3", "c3"),
    4: ("A4", "c4"),
}
ONE, TWO, THREE = (-1, -2), (0, -3, 1, 2), (3, 4)
EARLY, LATER = ("own", "pair", "ff", "sP+", "sP-", "sU+", "sU-"), ("sF-", "gP", "gF", "gU")
STAGES = (
    [(n, ONE) for n in EARLY],
    [(n, TWO) for n in EARLY] + [(n, ONE + TWO) for n in LATER],
    [(n, THREE) for n in EARLY + LATER] + [("sF+", ONE + TWO + THREE)],
)


def stage_kernel(work, names, before, last, *refs):
    n = len(names)
    place, arrays, o_ref = refs[0], dict(zip(names, refs[1 : 1 + n])), refs[-1 - last]
    acc = refs[-1]
    y, c, x, z = (place[i] for i in range(4))
    rows = arrays[PIECES[work[0][1][0]][0]].shape[-2]

    def pick(step, col):
        ref = arrays[PIECES[step][col]]
        return ref.at[1 - col] if len(ref.shape) == 4 else ref

    if before:
        acc[...] = refs[1 + n][...]
    else:
        acc[...] = jnp.zeros_like(acc)
    for name, steps in work:
        ref = arrays[name]
        a, b = STEPS[name]
        per = ref.shape[-1] // rows
        at_z = [lax.rem(z + (1 - 2 * c) * s + NZ, NZ) for s in steps]
        halves = [jnp.where(lax.div(f, per) == c, 0, 1) for f in at_z]
        lanes = [pl.multiple_of(lax.rem(f, per) * rows, rows) for f in at_z]

        def unit(u, _):
            along = 2 * u - 1 if a is None else a
            at_y = lax.rem(y + jnp.where(c == 0, along, b) + NY, NY)
            at_x = lax.rem(x + jnp.where(c == 0, b, along) + NX, NX)
            left = jnp.concatenate(
                [ref[u, h, :, pl.ds(at, rows)] for h, at in zip(halves, lanes)], axis=1
            )
            for col in range(NC):
                right = jnp.concatenate(
                    [pick(s, col)[at_y] for s in steps], axis=0
                )
                acc[col, at_x] += jnp.dot(
                    left, right, preferred_element_type=jnp.float32
                )
            return 0

        lax.fori_loop(0, ref.shape[0], unit, 0)
    if last:
        for col in range(NC):
            for i in range(NX):
                tokens, cols = acc.shape[2:]
                top = jnp.max(acc[col, i].reshape(tokens // LEN, LEN, cols), axis=1)
                o_ref[lax.rem(c + col, NC), i] = jnp.log1p(jnp.maximum(top, 0.0))


def run_stage(k, place, got):
    tokens = got["own"].shape[-2]
    cols = got["A0"].shape[-1]
    total = jax.ShapeDtypeStruct((NC, NX, tokens, cols), jnp.float32)
    result = jax.ShapeDtypeStruct((NC, NX, tokens // LEN, cols), jnp.float32)
    work = STAGES[k]
    names = list(dict.fromkeys(n for n, _ in work))
    names += list(dict.fromkeys(p for _, ss in work for s in ss for p in PIECES[s]))
    last = k == len(STAGES) - 1
    carried = [got["sum%d" % k]] if k else []

    def kernel(*refs):
        stage_kernel(work, names, k > 0, last, *refs)

    return pl.pallas_call(
        kernel,
        out_shape=result if last else total,
        in_specs=[SMEM] + [VMEM] * (len(names) + len(carried)),
        out_specs=VMEM,
        scratch_shapes=[pltpu.VMEM(total.shape, total.dtype)] if last else [],
        input_output_aliases={1 + len(names): 0} if carried and not last else {},
        compiler_params=pltpu.CompilerParams(vmem_limit_bytes=14 << 20),
    )(place, *(got[n] for n in names), *carried)


def body(hidden, head_weight, lengths):
    place = jnp.stack([lax.axis_index(a) for a in AXES]).astype(jnp.int32)
    kept, other, blocks = prep(place, lengths, hidden, head_weight)
    pooled = exchange(place, kept, other, blocks).astype(jnp.bfloat16)
    each = pooled.shape[-1] // NZ
    pooled = pooled.reshape(NC, NX * pooled.shape[2], NZ, each)
    pooled = jnp.transpose(pooled, (2, 0, 1, 3)).reshape(NZ * NC, -1, each)
    got = lax.all_to_all(pooled, ("z", "c"), split_axis=0, concat_axis=0, tiled=True)
    got = got.reshape(NZ, NC, NX, -1, each)
    got = jnp.transpose(got, (2, 0, 1, 3, 4)).reshape(-1, each).astype(jnp.float32)
    peak = jnp.max(got, axis=0)
    return jnp.transpose((got / (1.0 + peak)[None, :]).astype(jnp.bfloat16))


def solution(mesh):
    fine = Mesh(mesh.devices.reshape(SIZES), AXES)
    return jax.shard_map(
        body,
        mesh=fine,
        in_specs=(P(("x", "z"), ("y", "c")), P(("x", "z"), ("y", "c")), P(("x", "z"))),
        out_specs=P(("y", "c", "x", "z"), None),
        check_vma=False,
    )
```

```python
import jax
import jax.numpy as jnp
from jax import lax
from jax.experimental import pallas as pl
from jax.experimental.pallas import tpu as pltpu
from jax.sharding import Mesh, PartitionSpec as P

LEN = 64
AXES = ("y", "c", "x", "z")
NY, NC, NX, NZ = SIZES = (4, 2, 4, 8)
VMEM = pl.BlockSpec(memory_space=pltpu.VMEM)
SMEM = pl.BlockSpec(memory_space=pltpu.SMEM)


def permute(block, move):
    pairs = []
    for y in range(NY):
        for c in range(NC):
            for x in range(NX):
                for z in range(NZ):
                    to = [a % n for a, n in zip(move(y, c, x, z), SIZES)]
                    pairs.append(
                        (
                            ((y * NC + c) * NX + x) * NZ + z,
                            ((to[0] * NC + to[1]) * NX + to[2]) * NZ + to[3],
                        )
                    )
    return lax.ppermute(block, AXES, pairs)


def swap(block):
    return permute(block, lambda y, c, x, z: (y, 1 - c, x, z))


def first(block, s):
    return permute(
        block, lambda y, c, x, z: (y + s, c, x, z) if c == 0 else (y, c, x + s, z)
    )


def second(block, s):
    return permute(
        block, lambda y, c, x, z: (y, c, x + s, z) if c == 0 else (y + s, c, x, z)
    )


def along_z(block):
    return permute(
        block, lambda y, c, x, z: (y, c, x, z + 1) if c == 0 else (y, c, x, z - 1)
    )


def across_z(block):
    return permute(
        block, lambda y, c, x, z: (y, 0, x, z + 1) if c == 1 else (y, 1, x, z - 1)
    )


def prep_kernel(place, lengths, hid, head, kept, other, blocks):
    c = place[1]
    half, width = kept.shape[0], blocks.shape[2]
    for out, part in ((kept, c), (other, 1 - c)):
        for p in range(half // LEN):
            n = lengths[part * (half // LEN) + p]
            at = pl.multiple_of(part * half + p * LEN, LEN)
            rows = hid[pl.ds(at, LEN), :]
            j = lax.broadcasted_iota(jnp.int32, rows.shape, 0)
            zero = jnp.zeros_like(rows)
            out[p * LEN : (p + 1) * LEN, :] = jnp.where(j < n, rows, zero)
    for s in range(blocks.shape[0]):
        blocks[s] = head[:, s * width : (s + 1) * width]


def prep(place, lengths, hidden, head):
    rows, cols = head.shape
    half = jax.ShapeDtypeStruct((hidden.shape[0] // NC, hidden.shape[1]), hidden.dtype)
    blocks = jax.ShapeDtypeStruct((NX, rows, cols // NX), head.dtype)
    return pl.pallas_call(
        prep_kernel,
        out_shape=[half, half, blocks],
        in_specs=[SMEM, SMEM, VMEM, VMEM],
        out_specs=[VMEM] * 3,
        compiler_params=pltpu.CompilerParams(vmem_limit_bytes=6 << 20),
    )(place, lengths, hidden, head)


ORDER = (
    ("h0", ()),
    ("f+", ()),
    ("f-", ()),
    ("A1", ("f+", "f-")),
    ("B1", ("f+", "f-")),
    ("sP+", ()),
    ("sP-", ()),
    ("ff", ()),
    ("sU-", ()),
    ("sU+", ()),
    ("A2", ("sU+", "sU-")),
    ("B2", ()),
    ("sF-", ()),
    ("gP", ()),
    ("A3", ("sP+", "sP-", "ff")),
    ("B3", ()),
    ("B0", ("B2",)),
    ("c1", ()),
    ("gF", ()),
    ("sF+", ()),
    ("gU", ()),
    ("c2", ("gU",)),
    ("A4", ("sF-",)),
    ("c3", ("gP", "gF", "sum1", "c1")),
    ("c4", ("sF+", "c2", "c3", "sum2")),
)


def exchange(place, kept, other, blocks):
    got = {"kept": kept, "other": other}

    def own():
        if "own" not in got:
            got["own"] = jnp.stack([kept, got["h0"]])[None]
        return got["own"]

    def pair():
        if "pair" not in got:
            got["pair"] = jnp.concatenate([got["f+"], got["f-"]], axis=0)
        return got["pair"]

    def piece():
        if "A0" not in got:
            got["A0"] = lax.all_to_all(blocks, "x", split_axis=0, concat_axis=0)
        return got["A0"]

    moves = {
        "h0": (swap, lambda: other),
        "f+": (lambda b: first(b, 1), own),
        "f-": (lambda b: first(b, -1), own),
        "ff": (lambda b: first(b, 1), lambda: got["f+"]),
        "sU+": (lambda b: second(b, 1), own),
        "sU-": (lambda b: second(b, -1), own),
        "sP+": (lambda b: second(b, 1), pair),
        "sP-": (lambda b: second(b, -1), pair),
        "sF+": (lambda b: second(b, 1), lambda: got["ff"]),
        "sF-": (lambda b: second(b, -1), lambda: got["ff"]),
        "gU": (lambda b: second(b, -1), lambda: got["sU-"]),
        "gP": (lambda b: second(b, 1), lambda: got["sP+"]),
        "gF": (lambda b: second(b, -1), lambda: got["sF-"]),
        "B0": (swap, piece),
        "A1": (along_z, piece),
        "B1": (across_z, piece),
        "A2": (along_z, lambda: got["A1"]),
        "B2": (along_z, lambda: got["B1"]),
        "A3": (along_z, lambda: got["A2"]),
        "B3": (along_z, lambda: got["B2"]),
        "A4": (along_z, lambda: got["A3"]),
    }
    moves["c4"] = (swap, lambda: got["A4"])
    for n in "123":
        moves["c" + n] = (swap, lambda n=n: jnp.stack([got["A" + n], got["B" + n]]))
    for name, arrived in ORDER:
        for k in range(len(STAGES)):
            if "sum%d" % (k + 1) in arrived:
                got["sum%d" % (k + 1)] = run_stage(k, place, got)
        move, operand = moves[name]
        block = operand()
        if arrived:
            block = lax.optimization_barrier((block, *(got[a] for a in arrived)))[0]
        got[name] = move(block)
    for k in range(len(STAGES)):
        if "sum%d" % (k + 1) not in got:
            got["sum%d" % (k + 1)] = run_stage(k, place, got)
    return got["sum%d" % len(STAGES)]


STEPS = {
    "own": (0, 0),
    "sU+": (0, -1),
    "sU-": (0, 1),
    "pair": (None, 0),
    "ff": (2, 0),
    "gU": (0, 2),
    "sP+": (None, -1),
    "sP-": (None, 1),
    "sF+": (2, -1),
    "sF-": (2, 1),
    "gF": (2, 2),
    "gP": (None, 2),
}
PIECES = {
    0: ("A0", "B0"),
    -1: ("A1", "B1"),
    1: ("c1", "c1"),
    -2: ("A2", "B2"),
    2: ("c2", "c2"),
    -3: ("A3", "B3"),
    3: ("c3", "c3"),
    4: ("A4", "c4"),
}
ONE, TWO, THREE = (-1, -2), (0, -3, 1, 2), (3, 4)
EARLY, LATER = ("own", "pair", "ff", "sP+", "sP-", "sU+", "sU-"), ("sF-", "gP", "gF", "gU")
STAGES = (
    [(n, ONE) for n in EARLY],
    [(n, TWO) for n in EARLY] + [(n, ONE + TWO) for n in LATER],
    [(n, THREE) for n in EARLY + LATER] + [("sF+", ONE + TWO + THREE)],
)


def stage_kernel(work, names, before, last, *refs):
    n = len(names)
    place, arrays, o_ref = refs[0], dict(zip(names, refs[1 : 1 + n])), refs[-1 - last]
    acc = refs[-1]
    y, c, x, z = (place[i] for i in range(4))
    rows = arrays[PIECES[work[0][1][0]][0]].shape[-2]

    def pick(step, col):
        ref = arrays[PIECES[step][col]]
        return ref.at[1 - col] if len(ref.shape) == 4 else ref

    if before:
        acc[...] = refs[1 + n][...]
    else:
        acc[...] = jnp.zeros_like(acc)
    for name, steps in work:
        ref = arrays[name]
        a, b = STEPS[name]
        per = ref.shape[-1] // rows
        at_z = [lax.rem(z + (1 - 2 * c) * s + NZ, NZ) for s in steps]
        halves = [jnp.where(lax.div(f, per) == c, 0, 1) for f in at_z]
        lanes = [pl.multiple_of(lax.rem(f, per) * rows, rows) for f in at_z]

        def unit(u, _):
            along = 2 * u - 1 if a is None else a
            at_y = lax.rem(y + jnp.where(c == 0, along, b) + NY, NY)
            at_x = lax.rem(x + jnp.where(c == 0, b, along) + NX, NX)
            left = jnp.concatenate(
                [ref[u, h, :, pl.ds(at, rows)] for h, at in zip(halves, lanes)], axis=1
            )
            for col in range(NC):
                right = jnp.concatenate(
                    [pick(s, col)[at_y] for s in steps], axis=0
                )
                acc[col, at_x] += jnp.dot(
                    left, right, preferred_element_type=jnp.float32
                )
            return 0

        lax.fori_loop(0, ref.shape[0], unit, 0)
    if last:
        for col in range(NC):
            for i in range(NX):
                tokens, cols = acc.shape[2:]
                top = jnp.max(acc[col, i].reshape(tokens // LEN, LEN, cols), axis=1)
                o_ref[lax.rem(c + col, NC), i] = jnp.log1p(jnp.maximum(top, 0.0))


def run_stage(k, place, got):
    tokens = got["own"].shape[-2]
    cols = got["A0"].shape[-1]
    total = jax.ShapeDtypeStruct((NC, NX, tokens, cols), jnp.float32)
    result = jax.ShapeDtypeStruct((NC, NX, tokens // LEN, cols), jnp.float32)
    work = STAGES[k]
    names = list(dict.fromkeys(n for n, _ in work))
    names += list(dict.fromkeys(p for _, ss in work for s in ss for p in PIECES[s]))
    last = k == len(STAGES) - 1
    carried = [got["sum%d" % k]] if k else []

    def kernel(*refs):
        stage_kernel(work, names, k > 0, last, *refs)

    return pl.pallas_call(
        kernel,
        out_shape=result if last else total,
        in_specs=[SMEM] + [VMEM] * (len(names) + len(carried)),
        out_specs=VMEM,
        scratch_shapes=[pltpu.VMEM(total.shape, total.dtype)] if last else [],
        input_output_aliases={1 + len(names): 0} if carried and not last else {},
        compiler_params=pltpu.CompilerParams(vmem_limit_bytes=14 << 20),
    )(place, *(got[n] for n in names), *carried)


def body(hidden, head_weight, lengths):
    place = jnp.stack([lax.axis_index(a) for a in AXES]).astype(jnp.int32)
    kept, other, blocks = prep(place, lengths, hidden, head_weight)
    pooled = exchange(place, kept, other, blocks).astype(jnp.bfloat16)
    each = pooled.shape[-1] // NZ
    pooled = pooled.reshape(NC, NX * pooled.shape[2], NZ, each)
    pooled = jnp.transpose(pooled, (2, 0, 1, 3)).reshape(NZ * NC, -1, each)
    got = lax.all_to_all(pooled, ("z", "c"), split_axis=0, concat_axis=0, tiled=True)
    got = got.reshape(NZ, NC, NX, -1, each)
    got = jnp.transpose(got, (2, 0, 1, 3, 4)).reshape(-1, each).astype(jnp.float32)
    peak = jnp.max(got, axis=0)
    return jnp.transpose((got / (1.0 + peak)[None, :]).astype(jnp.bfloat16))


def solution(mesh):
    fine = Mesh(mesh.devices.reshape(SIZES), AXES)
    return jax.shard_map(
        body,
        mesh=fine,
        in_specs=(P(("x", "z"), ("y", "c")), P(("x", "z"), ("y", "c")), P(("x", "z"))),
        out_specs=P(("y", "c", "x", "z"), None),
        check_vma=False,
    )
```

```python
import jax
import jax.numpy as jnp
from jax import lax
from jax.experimental import pallas as pl
from jax.experimental.pallas import tpu as pltpu
from jax.sharding import Mesh, PartitionSpec as P

LEN = 64
AXES = ("y", "c", "x", "z")
NY, NC, NX, NZ = SIZES = (4, 2, 4, 8)
VMEM = pl.BlockSpec(memory_space=pltpu.VMEM)
SMEM = pl.BlockSpec(memory_space=pltpu.SMEM)


def permute(block, move):
    pairs = []
    for y in range(NY):
        for c in range(NC):
            for x in range(NX):
                for z in range(NZ):
                    to = [a % n for a, n in zip(move(y, c, x, z), SIZES)]
                    pairs.append(
                        (
                            ((y * NC + c) * NX + x) * NZ + z,
                            ((to[0] * NC + to[1]) * NX + to[2]) * NZ + to[3],
                        )
                    )
    return lax.ppermute(block, AXES, pairs)


def swap(block):
    return permute(block, lambda y, c, x, z: (y, 1 - c, x, z))


def first(block, s):
    return permute(
        block, lambda y, c, x, z: (y + s, c, x, z) if c == 0 else (y, c, x + s, z)
    )


def second(block, s):
    return permute(
        block, lambda y, c, x, z: (y, c, x + s, z) if c == 0 else (y + s, c, x, z)
    )


def along_z(block):
    return permute(
        block, lambda y, c, x, z: (y, c, x, z + 1) if c == 0 else (y, c, x, z - 1)
    )


def across_z(block):
    return permute(
        block, lambda y, c, x, z: (y, 0, x, z + 1) if c == 1 else (y, 1, x, z - 1)
    )


def prep_kernel(place, lengths, hid, head, kept, other, blocks):
    c = place[1]
    half, width = kept.shape[0], blocks.shape[2]
    for out, part in ((kept, c), (other, 1 - c)):
        for p in range(half // LEN):
            n = lengths[part * (half // LEN) + p]
            at = pl.multiple_of(part * half + p * LEN, LEN)
            rows = hid[pl.ds(at, LEN), :]
            j = lax.broadcasted_iota(jnp.int32, rows.shape, 0)
            zero = jnp.zeros_like(rows)
            out[p * LEN : (p + 1) * LEN, :] = jnp.where(j < n, rows, zero)
    for s in range(blocks.shape[0]):
        blocks[s] = head[:, s * width : (s + 1) * width]


def prep(place, lengths, hidden, head):
    rows, cols = head.shape
    half = jax.ShapeDtypeStruct((hidden.shape[0] // NC, hidden.shape[1]), hidden.dtype)
    blocks = jax.ShapeDtypeStruct((NX, rows, cols // NX), head.dtype)
    return pl.pallas_call(
        prep_kernel,
        out_shape=[half, half, blocks],
        in_specs=[SMEM, SMEM, VMEM, VMEM],
        out_specs=[VMEM] * 3,
    )(place, lengths, hidden, head)


ORDER = (
    ("h0", ()),
    ("f+", ()),
    ("f-", ()),
    ("A1", ("f+", "f-")),
    ("B1", ("f+", "f-")),
    ("sP+", ()),
    ("sP-", ()),
    ("ff", ()),
    ("sU-", ()),
    ("sU+", ()),
    ("A2", ("sU+", "sU-")),
    ("B2", ()),
    ("sF-", ()),
    ("gP", ()),
    ("A3", ("sP+", "sP-", "ff")),
    ("B3", ()),
    ("B0", ("B2",)),
    ("c1", ()),
    ("gF", ()),
    ("sF+", ()),
    ("gU", ()),
    ("c2", ("gU",)),
    ("A4", ("sF-",)),
    ("c3", ("gP", "gF", "sum1", "c1")),
    ("c4", ("sF+", "c2", "c3", "sum2")),
)


def exchange(place, kept, other, blocks):
    got = {"kept": kept, "other": other}

    def own():
        if "own" not in got:
            got["own"] = jnp.stack([kept, got["h0"]])[None]
        return got["own"]

    def pair():
        if "pair" not in got:
            got["pair"] = jnp.concatenate([got["f+"], got["f-"]], axis=0)
        return got["pair"]

    def piece():
        if "A0" not in got:
            got["A0"] = lax.all_to_all(blocks, "x", split_axis=0, concat_axis=0)
        return got["A0"]

    moves = {
        "h0": (swap, lambda: other),
        "f+": (lambda b: first(b, 1), own),
        "f-": (lambda b: first(b, -1), own),
        "ff": (lambda b: first(b, 1), lambda: got["f+"]),
        "sU+": (lambda b: second(b, 1), own),
        "sU-": (lambda b: second(b, -1), own),
        "sP+": (lambda b: second(b, 1), pair),
        "sP-": (lambda b: second(b, -1), pair),
        "sF+": (lambda b: second(b, 1), lambda: got["ff"]),
        "sF-": (lambda b: second(b, -1), lambda: got["ff"]),
        "gU": (lambda b: second(b, -1), lambda: got["sU-"]),
        "gP": (lambda b: second(b, 1), lambda: got["sP+"]),
        "gF": (lambda b: second(b, -1), lambda: got["sF-"]),
        "B0": (swap, piece),
        "A1": (along_z, piece),
        "B1": (across_z, piece),
        "A2": (along_z, lambda: got["A1"]),
        "B2": (along_z, lambda: got["B1"]),
        "A3": (along_z, lambda: got["A2"]),
        "B3": (along_z, lambda: got["B2"]),
        "A4": (along_z, lambda: got["A3"]),
    }
    moves["c4"] = (swap, lambda: got["A4"])
    for n in "123":
        moves["c" + n] = (swap, lambda n=n: jnp.stack([got["A" + n], got["B" + n]]))
    for name, arrived in ORDER:
        for k in range(len(STAGES)):
            if "sum%d" % (k + 1) in arrived:
                got["sum%d" % (k + 1)] = run_stage(k, place, got)
        move, operand = moves[name]
        block = operand()
        if arrived:
            block = lax.optimization_barrier((block, *(got[a] for a in arrived)))[0]
        got[name] = move(block)
    for k in range(len(STAGES)):
        if "sum%d" % (k + 1) not in got:
            got["sum%d" % (k + 1)] = run_stage(k, place, got)
    return got["sum%d" % len(STAGES)]


STEPS = {
    "own": (0, 0),
    "sU+": (0, -1),
    "sU-": (0, 1),
    "pair": (None, 0),
    "ff": (2, 0),
    "gU": (0, 2),
    "sP+": (None, -1),
    "sP-": (None, 1),
    "sF+": (2, -1),
    "sF-": (2, 1),
    "gF": (2, 2),
    "gP": (None, 2),
}
PIECES = {
    0: ("A0", "B0"),
    -1: ("A1", "B1"),
    1: ("c1", "c1"),
    -2: ("A2", "B2"),
    2: ("c2", "c2"),
    -3: ("A3", "B3"),
    3: ("c3", "c3"),
    4: ("A4", "c4"),
}
ONE, TWO, THREE = (-1, -2), (0, -3, 1, 2), (3, 4)
EARLY, LATER = ("own", "pair", "ff", "sP+", "sP-", "sU+", "sU-"), ("sF-", "gP", "gF", "gU")
STAGES = (
    [(n, ONE) for n in EARLY],
    [(n, TWO) for n in EARLY] + [(n, ONE + TWO) for n in LATER],
    [(n, THREE) for n in EARLY + LATER] + [("sF+", ONE + TWO + THREE)],
)


def stage_kernel(work, names, before, last, *refs):
    n = len(names)
    place, arrays, o_ref = refs[0], dict(zip(names, refs[1 : 1 + n])), refs[-1 - last]
    acc = refs[-1]
    y, c, x, z = (place[i] for i in range(4))
    rows = arrays[PIECES[work[0][1][0]][0]].shape[-2]

    def pick(step, col):
        ref = arrays[PIECES[step][col]]
        return ref.at[1 - col] if len(ref.shape) == 4 else ref

    if not before:
        acc[...] = jnp.zeros_like(acc)
    elif last:
        acc[...] = refs[1 + n][...]
    for name, steps in work:
        ref = arrays[name]
        a, b = STEPS[name]
        per = ref.shape[-1] // rows
        at_z = [lax.rem(z + (1 - 2 * c) * s + NZ, NZ) for s in steps]
        halves = [jnp.where(lax.div(f, per) == c, 0, 1) for f in at_z]
        lanes = [pl.multiple_of(lax.rem(f, per) * rows, rows) for f in at_z]

        def unit(u, _):
            along = 2 * u - 1 if a is None else a
            at_y = lax.rem(y + jnp.where(c == 0, along, b) + NY, NY)
            at_x = lax.rem(x + jnp.where(c == 0, b, along) + NX, NX)
            left = jnp.concatenate(
                [ref[u, h, :, pl.ds(at, rows)] for h, at in zip(halves, lanes)], axis=1
            )
            for col in range(NC):
                right = jnp.concatenate(
                    [pick(s, col)[at_y] for s in steps], axis=0
                )
                acc[col, at_x] += jnp.dot(
                    left, right, preferred_element_type=jnp.float32
                )
            return 0

        lax.fori_loop(0, ref.shape[0], unit, 0)
    if last:
        for col in range(NC):
            for i in range(NX):
                tokens, cols = acc.shape[2:]
                top = jnp.max(acc[col, i].reshape(tokens // LEN, LEN, cols), axis=1)
                o_ref[lax.rem(c + col, NC), i] = jnp.log1p(jnp.maximum(top, 0.0))


def run_stage(k, place, got):
    tokens = got["own"].shape[-2]
    cols = got["A0"].shape[-1]
    total = jax.ShapeDtypeStruct((NC, NX, tokens, cols), jnp.float32)
    result = jax.ShapeDtypeStruct((NC, NX, tokens // LEN, cols), jnp.float32)
    work = STAGES[k]
    names = list(dict.fromkeys(n for n, _ in work))
    names += list(dict.fromkeys(p for _, ss in work for s in ss for p in PIECES[s]))
    last = k == len(STAGES) - 1
    carried = [got["sum%d" % k]] if k else []

    def kernel(*refs):
        stage_kernel(work, names, k > 0, last, *refs)

    return pl.pallas_call(
        kernel,
        out_shape=result if last else total,
        in_specs=[SMEM] + [VMEM] * (len(names) + len(carried)),
        out_specs=VMEM,
        scratch_shapes=[pltpu.VMEM(total.shape, total.dtype)] if last else [],
        input_output_aliases={1 + len(names): 0} if carried and not last else {},
        compiler_params=pltpu.CompilerParams(vmem_limit_bytes=14 << 20),
    )(place, *(got[n] for n in names), *carried)


def body(hidden, head_weight, lengths):
    place = jnp.stack([lax.axis_index(a) for a in AXES]).astype(jnp.int32)
    kept, other, blocks = prep(place, lengths, hidden, head_weight)
    pooled = exchange(place, kept, other, blocks).astype(jnp.bfloat16)
    each = pooled.shape[-1] // NZ
    pooled = pooled.reshape(NC, NX * pooled.shape[2], NZ, each)
    pooled = jnp.transpose(pooled, (2, 0, 1, 3)).reshape(NZ * NC, -1, each)
    got = lax.all_to_all(pooled, ("z", "c"), split_axis=0, concat_axis=0, tiled=True)
    got = got.reshape(NZ, NC, NX, -1, each)
    got = jnp.transpose(got, (2, 0, 1, 3, 4)).reshape(-1, each).astype(jnp.float32)
    peak = jnp.max(got, axis=0)
    return jnp.transpose((got / (1.0 + peak)[None, :]).astype(jnp.bfloat16))


def solution(mesh):
    fine = Mesh(mesh.devices.reshape(SIZES), AXES)
    return jax.shard_map(
        body,
        mesh=fine,
        in_specs=(P(("x", "z"), ("y", "c")), P(("x", "z"), ("y", "c")), P(("x", "z"))),
        out_specs=P(("y", "c", "x", "z"), None),
        check_vma=False,
    )
```

```python
import jax
import jax.numpy as jnp
from jax import lax
from jax.experimental import pallas as pl
from jax.experimental.pallas import tpu as pltpu
from jax.sharding import Mesh, PartitionSpec as P

LEN = 64
AXES = ("y", "c", "x", "z")
NY, NC, NX, NZ = SIZES = (4, 2, 4, 8)
VMEM = pl.BlockSpec(memory_space=pltpu.VMEM)
SMEM = pl.BlockSpec(memory_space=pltpu.SMEM)


def permute(block, move):
    pairs = []
    for y in range(NY):
        for c in range(NC):
            for x in range(NX):
                for z in range(NZ):
                    to = [a % n for a, n in zip(move(y, c, x, z), SIZES)]
                    pairs.append(
                        (
                            ((y * NC + c) * NX + x) * NZ + z,
                            ((to[0] * NC + to[1]) * NX + to[2]) * NZ + to[3],
                        )
                    )
    return lax.ppermute(block, AXES, pairs)


def swap(block):
    return permute(block, lambda y, c, x, z: (y, 1 - c, x, z))


def first(block, s):
    return permute(
        block, lambda y, c, x, z: (y + s, c, x, z) if c == 0 else (y, c, x + s, z)
    )


def second(block, s):
    return permute(
        block, lambda y, c, x, z: (y, c, x + s, z) if c == 0 else (y + s, c, x, z)
    )


def along_z(block):
    return permute(
        block, lambda y, c, x, z: (y, c, x, z + 1) if c == 0 else (y, c, x, z - 1)
    )


def across_z(block):
    return permute(
        block, lambda y, c, x, z: (y, 0, x, z + 1) if c == 1 else (y, 1, x, z - 1)
    )


def prep_kernel(place, lengths, hid, head, kept, other, blocks):
    c = place[1]
    half, width = kept.shape[0], blocks.shape[2]
    for out, part in ((kept, c), (other, 1 - c)):
        for p in range(half // LEN):
            n = lengths[part * (half // LEN) + p]
            at = pl.multiple_of(part * half + p * LEN, LEN)
            rows = hid[pl.ds(at, LEN), :]
            j = lax.broadcasted_iota(jnp.int32, rows.shape, 0)
            zero = jnp.zeros_like(rows)
            out[p * LEN : (p + 1) * LEN, :] = jnp.where(j < n, rows, zero)
    for s in range(blocks.shape[0]):
        blocks[s] = head[:, s * width : (s + 1) * width]


def prep(place, lengths, hidden, head):
    rows, cols = head.shape
    half = jax.ShapeDtypeStruct((hidden.shape[0] // NC, hidden.shape[1]), hidden.dtype)
    blocks = jax.ShapeDtypeStruct((NX, rows, cols // NX), head.dtype)
    return pl.pallas_call(
        prep_kernel,
        out_shape=[half, half, blocks],
        in_specs=[SMEM, SMEM, VMEM, VMEM],
        out_specs=[VMEM] * 3,
    )(place, lengths, hidden, head)


ORDER = (
    ("h0", ()),
    ("f+", ()),
    ("f-", ()),
    ("A1", ("f+", "f-")),
    ("B1", ("f+", "f-")),
    ("sP+", ()),
    ("sP-", ()),
    ("ff", ()),
    ("sU-", ()),
    ("sU+", ()),
    ("A2", ("sU+", "sU-")),
    ("B2", ()),
    ("sF-", ()),
    ("gP", ()),
    ("A3", ("sP+", "sP-", "ff")),
    ("B3", ()),
    ("B0", ("B2",)),
    ("c1", ()),
    ("gF", ()),
    ("sF+", ()),
    ("gU", ()),
    ("c2", ("gU",)),
    ("A4", ("sF-",)),
    ("c3", ("gP", "gF", "sum1", "c1")),
    ("c4", ("sF+", "c2", "c3", "sum2")),
)


def exchange(place, kept, other, blocks):
    got = {"kept": kept, "other": other}

    def own():
        if "own" not in got:
            got["own"] = jnp.stack([kept, got["h0"]])[None]
        return got["own"]

    def pair():
        if "pair" not in got:
            got["pair"] = jnp.concatenate([got["f+"], got["f-"]], axis=0)
        return got["pair"]

    def piece():
        if "A0" not in got:
            got["A0"] = lax.all_to_all(blocks, "x", split_axis=0, concat_axis=0)
        return got["A0"]

    moves = {
        "h0": (swap, lambda: other),
        "f+": (lambda b: first(b, 1), own),
        "f-": (lambda b: first(b, -1), own),
        "ff": (lambda b: first(b, 1), lambda: got["f+"]),
        "sU+": (lambda b: second(b, 1), own),
        "sU-": (lambda b: second(b, -1), own),
        "sP+": (lambda b: second(b, 1), pair),
        "sP-": (lambda b: second(b, -1), pair),
        "sF+": (lambda b: second(b, 1), lambda: got["ff"]),
        "sF-": (lambda b: second(b, -1), lambda: got["ff"]),
        "gU": (lambda b: second(b, -1), lambda: got["sU-"]),
        "gP": (lambda b: second(b, 1), lambda: got["sP+"]),
        "gF": (lambda b: second(b, -1), lambda: got["sF-"]),
        "B0": (swap, piece),
        "A1": (along_z, piece),
        "B1": (across_z, piece),
        "A2": (along_z, lambda: got["A1"]),
        "B2": (along_z, lambda: got["B1"]),
        "A3": (along_z, lambda: got["A2"]),
        "B3": (along_z, lambda: got["B2"]),
        "A4": (along_z, lambda: got["A3"]),
    }
    moves["c4"] = (swap, lambda: got["A4"])
    for n in "123":
        moves["c" + n] = (swap, lambda n=n: jnp.stack([got["A" + n], got["B" + n]]))
    for name, arrived in ORDER:
        for k in range(len(STAGES)):
            if "sum%d" % (k + 1) in arrived:
                got["sum%d" % (k + 1)] = run_stage(k, place, got)
        move, operand = moves[name]
        block = operand()
        if arrived:
            block = lax.optimization_barrier((block, *(got[a] for a in arrived)))[0]
        got[name] = move(block)
    for k in range(len(STAGES)):
        if "sum%d" % (k + 1) not in got:
            got["sum%d" % (k + 1)] = run_stage(k, place, got)
    return got["sum%d" % len(STAGES)]


STEPS = {
    "own": (0, 0),
    "sU+": (0, -1),
    "sU-": (0, 1),
    "pair": (None, 0),
    "ff": (2, 0),
    "gU": (0, 2),
    "sP+": (None, -1),
    "sP-": (None, 1),
    "sF+": (2, -1),
    "sF-": (2, 1),
    "gF": (2, 2),
    "gP": (None, 2),
}
PIECES = {
    0: ("A0", "B0"),
    -1: ("A1", "B1"),
    1: ("c1", "c1"),
    -2: ("A2", "B2"),
    2: ("c2", "c2"),
    -3: ("A3", "B3"),
    3: ("c3", "c3"),
    4: ("A4", "c4"),
}
ONE, TWO, THREE = (-1, -2), (0, -3, 1, 2), (3, 4)
EARLY, LATER = ("own", "pair", "ff", "sP+", "sP-", "sU+", "sU-"), ("sF-", "gP", "gF", "gU")
STAGES = (
    [(n, ONE) for n in EARLY],
    [(n, TWO) for n in EARLY] + [(n, ONE + TWO) for n in LATER],
    [(n, THREE) for n in EARLY + LATER] + [("sF+", ONE + TWO + THREE)],
)


def stage_kernel(work, names, before, last, *refs):
    n = len(names)
    place, arrays, o_ref = refs[0], dict(zip(names, refs[1 : 1 + n])), refs[-1 - last]
    acc = refs[-1]
    y, c, x, z = (place[i] for i in range(4))
    rows = arrays[PIECES[work[0][1][0]][0]].shape[-2]

    def pick(step, col):
        ref = arrays[PIECES[step][col]]
        return ref.at[1 - col] if len(ref.shape) == 4 else ref

    if not before:
        acc[...] = jnp.zeros_like(acc)
    elif last:
        acc[...] = refs[1 + n][...]
    for name, steps in work:
        ref = arrays[name]
        a, b = STEPS[name]
        per = ref.shape[-1] // rows
        at_z = [lax.rem(z + (1 - 2 * c) * s + NZ, NZ) for s in steps]
        halves = [jnp.where(lax.div(f, per) == c, 0, 1) for f in at_z]
        lanes = [pl.multiple_of(lax.rem(f, per) * rows, rows) for f in at_z]

        def unit(u, _):
            along = 2 * u - 1 if a is None else a
            at_y = lax.rem(y + jnp.where(c == 0, along, b) + NY, NY)
            at_x = lax.rem(x + jnp.where(c == 0, b, along) + NX, NX)
            left = jnp.concatenate(
                [ref[u, h, :, pl.ds(at, rows)] for h, at in zip(halves, lanes)], axis=1
            )
            for col in range(NC):
                right = jnp.concatenate(
                    [pick(s, col)[at_y] for s in steps], axis=0
                )
                acc[col, at_x] += jnp.dot(
                    left, right, preferred_element_type=jnp.float32
                )
            return 0

        lax.fori_loop(0, ref.shape[0], unit, 0)
    if last:
        for col in range(NC):
            for i in range(NX):
                tokens, cols = acc.shape[2:]
                top = jnp.max(acc[col, i].reshape(tokens // LEN, LEN, cols), axis=1)
                o_ref[lax.rem(c + col, NC), i] = jnp.log1p(jnp.maximum(top, 0.0))


def run_stage(k, place, got):
    tokens = got["own"].shape[-2]
    cols = got["A0"].shape[-1]
    total = jax.ShapeDtypeStruct((NC, NX, tokens, cols), jnp.float32)
    result = jax.ShapeDtypeStruct((NC, NX, tokens // LEN, cols), jnp.float32)
    work = STAGES[k]
    names = list(dict.fromkeys(n for n, _ in work))
    names += list(dict.fromkeys(p for _, ss in work for s in ss for p in PIECES[s]))
    last = k == len(STAGES) - 1
    carried = [got["sum%d" % k]] if k else []

    def kernel(*refs):
        stage_kernel(work, names, k > 0, last, *refs)

    return pl.pallas_call(
        kernel,
        out_shape=result if last else total,
        in_specs=[SMEM] + [VMEM] * (len(names) + len(carried)),
        out_specs=VMEM,
        scratch_shapes=[pltpu.VMEM(total.shape, total.dtype)] if last else [],
        input_output_aliases={1 + len(names): 0} if carried and not last else {},
        compiler_params=pltpu.CompilerParams(vmem_limit_bytes=14 << 20),
    )(place, *(got[n] for n in names), *carried)


def finish_kernel(got, out):
    values = got[...].astype(jnp.float32)
    peak = jnp.max(jnp.max(values, axis=0), axis=0, keepdims=True)
    per = values.shape[1] // NX
    scaled = values / (1.0 + peak)[None]
    rows = [scaled[:, x * per : (x + 1) * per, :] for x in range(NX)]
    rows = [r.reshape(-1, r.shape[-1]) for r in rows]
    out[...] = jnp.transpose(jnp.concatenate(rows, axis=0)).astype(out.dtype)


def finish(got):
    shape = (got.shape[2], got.shape[0] * got.shape[1])
    return pl.pallas_call(
        finish_kernel,
        out_shape=jax.ShapeDtypeStruct(shape, got.dtype),
        in_specs=[VMEM],
        out_specs=VMEM,
    )(got)


def body(hidden, head_weight, lengths):
    place = jnp.stack([lax.axis_index(a) for a in AXES]).astype(jnp.int32)
    kept, other, blocks = prep(place, lengths, hidden, head_weight)
    pooled = exchange(place, kept, other, blocks).astype(jnp.bfloat16)
    each = pooled.shape[-1] // NZ
    pooled = pooled.reshape(NC, NX * pooled.shape[2], NZ, each)
    pooled = jnp.transpose(pooled, (2, 0, 1, 3)).reshape(NZ * NC, -1, each)
    got = lax.all_to_all(pooled, ("z", "c"), split_axis=0, concat_axis=0, tiled=True)
    return finish(got)


def solution(mesh):
    fine = Mesh(mesh.devices.reshape(SIZES), AXES)
    return jax.shard_map(
        body,
        mesh=fine,
        in_specs=(P(("x", "z"), ("y", "c")), P(("x", "z"), ("y", "c")), P(("x", "z"))),
        out_specs=P(("y", "c", "x", "z"), None),
        check_vma=False,
    )
```
